256 devices in a mesh: ctx: 64 (over z, x, y_lo), head: 4 (over y_hi, core).
Axes of the slice: x: 4, y: 4 (y_hi: 2, y_lo: 2; y = y_hi * 2 + y_lo), z: 8, core: 2. Of those that a mesh axis runs over, the one named last changes fastest.
Arguments:
- queries: bfloat16 [8192, 2048], P(('ctx', 'head')), as said below
- key_rows: bfloat16 [8192, 512], P(('ctx', 'head')), as said below
- value_rows: bfloat16 [8192, 512], P(('ctx', 'head')), may hold values from -6 to 6
- query_tangent: bfloat16 [8192, 2048], P(('ctx', 'head')), may hold values from -6 to 6
- key_tangent: bfloat16 [8192, 512], P(('ctx', 'head')), may hold values from -6 to 6
- value_tangent: bfloat16 [8192, 512], P(('ctx', 'head')), may hold values from -6 to 6
- block_plan: int32 [64], replicated, may hold values from 0 to 63, each once
- block_docs: int32 [64], replicated, may hold values from 0 to 15, never falling along the last dimension, each value on 1 to 8 neighbouring positions
Outputs:
- attended: bfloat16 [8192, 2048], P(('ctx', 'head'))
- attended_tangent: bfloat16 [8192, 2048], P(('ctx', 'head'))
The draws below stay inside these ranges and needn't reach their ends.
Inputs may be any that keep to these rules, and one draw needn't show every extreme that they name: `block_plan`: each packed block holds a different context block. `block_docs`: ids never fall along the context; each document covers 1 to 8 blocks, one exactly 8. `queries`: entries lie within -6 and 6. `key_rows`: entries lie within -6 and 6.
All inputs are finite; a program needn't handle non-finite values.
Results may differ from the reference program's by a relative error of at most 0.0083.
Values may be sent and summed in bfloat16 or wider, within the bound.
No kernel may reach another device: no remote copies, remote signals or barrier semaphores. Data moves between devices by JAX's collectives and lax.ppermute only.
A program may use at most 128 MiB of HBM per device.

```python
import math
import jax
import jax.numpy as jnp
import numpy as np
from jax import lax

HD = 128
HQ = 16
KVH = 4
BLK = 128
TOKENS = 8192
NBLK = 64
DOCS = 16
DOC_MOST = 8


def draw_queries(key, part):
    base = jnp.clip(jax.random.normal(jax.random.fold_in(key, 11), (TOKENS, HQ * HD), jnp.float32), -6.0, 6.0)
    return base.astype(jnp.bfloat16)


def draw_key_rows(key, part):
    base = jnp.clip(jax.random.normal(jax.random.fold_in(key, 12), (TOKENS, KVH * HD), jnp.float32), -6.0, 6.0)
    return base.astype(jnp.bfloat16)


def shard_levels(key, dims, pieces, low, high):
    def one(axis_at, shards_of):
        steps = jax.random.uniform(jax.random.fold_in(jax.random.fold_in(key, 6), axis_at), (shards_of,), jnp.float32, low / len(pieces), high / len(pieces))
        return jnp.repeat(jnp.exp(steps), dims[axis_at] // shards_of).reshape((-1,) + (1,) * (len(dims) - axis_at - 1))

    gain = one(*pieces[0])
    for cut in pieces[1:]:
        gain = gain * one(*cut)
    return gain


def split_up(count, total, limit, slope):
    portions = [(1 << 20) // math.isqrt(standing ** slope) + 1 for standing in range(2, count + 1)]
    surplus, given = total - limit - (count - 1), [1] * (count - 1)
    while surplus > 0:
        free = [i for i in range(count - 1) if given[i] < limit]
        whole, remaining = sum([portions[i] for i in free]), surplus
        for i in free:
            more = min(limit - given[i], max(1, remaining * portions[i] // whole), surplus)
            given[i] = given[i] + more
            surplus = surplus - more
    return np.array([limit] + given)


def ragged(key, count, total, most, lean):
    if count == 2:
        one = jax.random.randint(key, (), max(1, total - most), min(most, total - 1) + 1)
        return jnp.stack([one, total - one])
    tallies = jnp.asarray(split_up(count, total, most, lean), jnp.int32)
    pairs = (count - 1) // 2
    donor, taker = tallies[1:1 + 2 * pairs:2], tallies[2:2 + 2 * pairs:2]
    slack = jnp.minimum(donor - 1, most - taker)
    shifted = jax.random.randint(jax.random.fold_in(key, 1), (pairs,), 0, 1 << 20) % (slack + 1)
    tallies = tallies.at[1:1 + 2 * pairs:2].set(donor - shifted).at[2:2 + 2 * pairs:2].set(taker + shifted)
    return tallies[jax.random.permutation(jax.random.fold_in(key, 2), count)]


def gaussian(own_key, extent, width, limit, cuts=(), kind=jnp.bfloat16):
    level = shard_levels(own_key, extent, cuts, -0.22, 0.18) if cuts else 1.0
    entries = jax.random.normal(own_key, extent, jnp.float32) * width * level
    return jnp.minimum(jnp.maximum(entries, -limit), limit).astype(kind)


def setup_inputs(seed: int = 0) -> dict:
    key_of = jax.random.split(jax.random.key(seed), 9)
    queries = draw_queries(jax.random.fold_in(key_of[8], 71), 0)
    key_rows = draw_key_rows(jax.random.fold_in(key_of[8], 71), 0)
    value_rows = gaussian(key_of[2], (TOKENS, KVH * HD), 1.0, 6.0, ((0, 256),))
    query_tangent = gaussian(key_of[3], (TOKENS, HQ * HD), 1.0, 6.0, ((0, 256),))
    key_tangent = gaussian(key_of[4], (TOKENS, KVH * HD), 1.0, 6.0, ((0, 256),))
    value_tangent = gaussian(key_of[5], (TOKENS, KVH * HD), 1.0, 6.0, ((0, 256),))
    block_plan = jax.random.permutation(key_of[6], NBLK).astype(jnp.int32)
    block_docs = jnp.searchsorted(jnp.cumsum(ragged(key_of[7], DOCS, NBLK, DOC_MOST, 2)), jnp.arange(NBLK), side="right").astype(jnp.int32)
    return {"queries": queries, "key_rows": key_rows, "value_rows": value_rows, "query_tangent": query_tangent, "key_tangent": key_tangent, "value_tangent": value_tangent, "block_plan": block_plan, "block_docs": block_docs}


def reference(queries, key_rows, value_rows, query_tangent, key_tangent, value_tangent, block_plan, block_docs):
    scale = 1.0 / math.sqrt(HD)
    group = HQ // KVH
    window = DOC_MOST
    inverse = jnp.zeros((NBLK,), jnp.int32).at[block_plan].set(jnp.arange(NBLK, dtype=jnp.int32))

    def to_context(array):
        return array.reshape(NBLK, BLK, -1)[inverse]

    def padded(array):
        blocks = to_context(array).reshape(NBLK, BLK, KVH, HD)
        front = jnp.zeros((window - 1, BLK, KVH, HD), blocks.dtype)
        return jnp.concatenate([front, blocks], axis=0)
    query_ctx = to_context(queries).reshape(NBLK, BLK, KVH, group, HD)
    qtan_ctx = to_context(query_tangent).reshape(NBLK, BLK, KVH, group, HD)
    key_pad = padded(key_rows)
    value_pad = padded(value_rows)
    ktan_pad = padded(key_tangent)
    vtan_pad = padded(value_tangent)
    docs_pad = jnp.concatenate([jnp.full((window - 1,), -1, jnp.int32), block_docs.astype(jnp.int32)])

    def one_block(index):

        def cut(array):
            return lax.dynamic_slice_in_dim(array, index, window, 0).reshape(window * BLK, KVH, HD).astype(jnp.float32)
        keys = cut(key_pad)
        values = cut(value_pad)
        ktan = cut(ktan_pad)
        vtan = cut(vtan_pad)
        kdoc = jnp.repeat(lax.dynamic_slice_in_dim(docs_pad, index, window, 0), BLK)
        kpos = (index - (window - 1)) * BLK + jnp.arange(window * BLK, dtype=jnp.int32)
        qpos = index * BLK + jnp.arange(BLK, dtype=jnp.int32)
        mask = (kdoc[None, :] == block_docs[index]) & (kpos[None, :] <= qpos[:, None])
        query = query_ctx[index].astype(jnp.float32)
        qtan = qtan_ctx[index].astype(jnp.float32)
        score = jnp.einsum('qhgd,khd->hgqk', query, keys) * scale
        dscore = (jnp.einsum('qhgd,khd->hgqk', qtan, keys) + jnp.einsum('qhgd,khd->hgqk', query, ktan)) * scale
        masked = jnp.where(mask, score, -1e+30)
        top = lax.optimization_barrier(jnp.max(masked, axis=-1, keepdims=True))
        weight = jnp.where(mask, jnp.exp(masked - top), 0.0)
        total = lax.optimization_barrier(jnp.sum(weight, axis=-1))
        curve = lax.optimization_barrier(jnp.sum(weight * dscore, axis=-1))
        weight_b = weight.astype(jnp.bfloat16).astype(jnp.float32)
        wds_b = (weight * dscore).astype(jnp.bfloat16).astype(jnp.float32)
        acc_a = jnp.einsum('hgqk,khd->qhgd', weight_b, values)
        acc_b = jnp.einsum('hgqk,khd->qhgd', wds_b, values) + jnp.einsum('hgqk,khd->qhgd', weight_b, vtan)
        total_q = jnp.transpose(total, (2, 0, 1))[..., None]
        curve_q = jnp.transpose(curve, (2, 0, 1))[..., None]
        output = acc_a / total_q
        tangent = acc_b / total_q - curve_q / total_q * output
        return (output.astype(jnp.bfloat16).reshape(BLK, HQ * HD), tangent.astype(jnp.bfloat16).reshape(BLK, HQ * HD))
    outputs, tangents = lax.map(one_block, jnp.arange(NBLK, dtype=jnp.int32))
    return (outputs[block_plan].reshape(TOKENS, HQ * HD), tangents[block_plan].reshape(TOKENS, HQ * HD))
```

```python
import functools
import math

import jax
import jax.numpy as jnp
from jax import lax
from jax.experimental import pallas as pl
from jax.experimental.pallas import tpu as pltpu
from jax.sharding import PartitionSpec as P

HD = 128
BLK = 128
SHARDS = 64
PIECES = 16
WINDOW = 8
NEG = -1e30
SCALE = 1.0 / math.sqrt(HD)
LOG2E = math.log2(math.e)
BF = jnp.bfloat16
F32 = jnp.float32
VMEM = pl.BlockSpec(memory_space=pltpu.VMEM)
SMEM = pl.BlockSpec(memory_space=pltpu.SMEM)


def lanes(start, size):
    return pl.ds(pl.multiple_of(start, 128), size)


def pack_keys(k, v, dk, dv, keep, send):
    core = lax.axis_index("head") % 2
    for y in range(2):
        for a, ref in enumerate((k, v, dk, dv)):
            keep[y, a] = ref[:, lanes((2 * y + core) * HD, HD)]
            send[y, a] = ref[:, lanes((2 * y + 1 - core) * HD, HD)]


def pack_queries(q, dq, own, to1, to2, to3):
    h = lax.axis_index("head")
    for j, out in enumerate((own, to1, to2, to3)):
        at = lanes(lax.bitwise_xor(h, j) * 512, 512)
        out[0] = q[:, at]
        out[1] = dq[:, at]


def spread(keep, got, out):
    core = lax.axis_index("head") % 2
    for y in range(2):
        for a in range(4):
            for r in range(4):
                rows = pl.ds(16 * (r % 2), 16)
                mine, other = keep[y, a, rows], got[y, a, rows]
                piece = jnp.where(core == r // 2, mine, other)
                for group in range(SHARDS // PIECES):
                    out[group * PIECES + a * 4 + r, y] = piece


def select(plan, docs, pieces, out, inverse):
    @pl.loop(0, SHARDS)
    def _(i):
        inverse[plan[i]] = i

    group = lax.axis_index("ctx") // PIECES
    for d in range(PIECES):
        t = plan[group * PIECES + d]
        for s in range(WINDOW):
            if s == 0:
                source = group * PIECES + d
            else:
                back = jnp.maximum(t - s, 0)
                same = jnp.logical_and(t >= s, docs[back] == docs[t])
                source = inverse[jnp.where(same, back, t)]
            out[d, s] = pieces[source]


def attend(plan, docs, q0, q1, q2, q3, keys, o0, o1, o2, o3):
    h = lax.axis_index("head")
    t = plan[lax.axis_index("ctx")]
    doc = docs[t]

    def gathered(a):
        return jnp.concatenate(
            [keys[a * 4 + r, s, y] for s in range(WINDOW) for y in range(2) for r in range(4)], axis=0
        )

    kk, vv, dkk, dvv = (gathered(a) for a in range(4))
    kdk = jnp.concatenate([kk, dkk], axis=1)
    vdv = jnp.concatenate([vv, dvv], axis=1)
    seen = []
    for s in range(1, WINDOW):
        back = jnp.maximum(t - s, 0)
        seen.append(jnp.logical_and(t >= s, docs[back] == doc))
    contract_last = (((1,), (1,)), ((), ()))
    for j, (q, o) in enumerate(((q0, o0), (q1, o1), (q2, o2), (q3, o3))):
        qa = jnp.concatenate([q[0, :, g * HD : (g + 1) * HD] for g in range(4)], axis=0)
        dqa = jnp.concatenate([q[1, :, g * HD : (g + 1) * HD] for g in range(4)], axis=0)
        score = lax.dot_general(qa, kk, contract_last, preferred_element_type=F32)
        dscore = lax.dot_general(
            jnp.concatenate([dqa, qa], axis=1), kdk, contract_last, preferred_element_type=F32
        )
        row = lax.broadcasted_iota(jnp.int32, (128, 128), 0) % 32 + 32 * lax.bitwise_xor(h, j)
        col = lax.broadcasted_iota(jnp.int32, (128, 128), 1)
        parts = [jnp.where(col <= row, score[:, :BLK], NEG)]
        for s in range(1, WINDOW):
            parts.append(jnp.where(seen[s - 1], score[:, s * BLK : (s + 1) * BLK], NEG))
        masked = jnp.concatenate(parts, axis=1)
        top = jnp.max(masked, axis=1, keepdims=True)
        weight = jnp.exp2((masked - top) * (SCALE * LOG2E))
        total = jnp.sum(weight, axis=1, keepdims=True)
        wds = weight * dscore
        curve = jnp.sum(wds, axis=1, keepdims=True) * SCALE
        ab = jnp.dot(weight.astype(BF), vdv, preferred_element_type=F32)
        b1 = jnp.dot(wds.astype(BF), vv, preferred_element_type=F32)
        inv = 1.0 / total
        a = ab[:, :HD] * inv
        b = (b1 * SCALE + ab[:, HD:]) * inv - (curve * inv) * a
        ab_, bb_ = a.astype(BF), b.astype(BF)
        for g in range(4):
            o[0, :, g * HD : (g + 1) * HD] = ab_[g * 32 : (g + 1) * 32]
            o[1, :, g * HD : (g + 1) * HD] = bb_[g * 32 : (g + 1) * 32]


def place(r0, r1, r2, r3, att, tan):
    h = lax.axis_index("head")
    for j, r in enumerate((r0, r1, r2, r3)):
        at = lanes(lax.bitwise_xor(h, j) * 512, 512)
        att[:, at] = r[0]
        tan[:, at] = r[1]


def struct(*shape):
    return jax.ShapeDtypeStruct(shape, BF)


def to_head(value, j):
    return lax.ppermute(value, "head", [(i, i ^ j) for i in range(4)])


def on_device(queries, key_rows, value_rows, query_tangent, key_tangent, value_tangent, plan, docs):
    keep, send = pl.pallas_call(
        pack_keys, out_shape=(struct(2, 4, 32, 128),) * 2, in_specs=[VMEM] * 4, out_specs=(VMEM,) * 2, name="pack_keys"
    )(key_rows, value_rows, key_tangent, value_tangent)
    got = to_head(send, 1)
    pieces = pl.pallas_call(
        spread, out_shape=struct(SHARDS, 2, 16, 128), in_specs=[VMEM] * 2, out_specs=VMEM, name="spread"
    )(keep, got)
    by_y = [[c * 4 + 2 * y + core for c in range(SHARDS) for y in range(2)] for core in range(2)]
    pieces = lax.all_to_all(
        pieces.reshape(SHARDS * 2, 16, 128), ("ctx", "head"), 0, 0, tiled=True, axis_index_groups=by_y
    ).reshape(SHARDS, 2, 16, 128)
    qs = pl.pallas_call(
        pack_queries, out_shape=(struct(2, 32, 512),) * 4, in_specs=[VMEM] * 2, out_specs=(VMEM,) * 4, name="pack_queries"
    )(queries, query_tangent)
    qs = [qs[0]] + [to_head(qs[j], j) for j in (1, 2, 3)]
    chosen = pl.pallas_call(
        select,
        out_shape=struct(PIECES, WINDOW, 2, 16, 128),
        in_specs=[SMEM, SMEM, VMEM],
        out_specs=VMEM,
        scratch_shapes=[pltpu.SMEM((SHARDS,), jnp.int32)],
        name="select",
    )(plan, docs, pieces)
    groups = [[g * PIECES + i for i in range(PIECES)] for g in range(SHARDS // PIECES)]
    chosen = lax.all_to_all(
        chosen.reshape(PIECES, WINDOW * 32, 128), "ctx", 0, 0, tiled=True, axis_index_groups=groups
    ).reshape(PIECES, WINDOW, 2, 16, 128)
    outs = pl.pallas_call(
        attend,
        out_shape=(struct(2, 32, 512),) * 4,
        in_specs=[SMEM, SMEM] + [VMEM] * 5,
        out_specs=(VMEM,) * 4,
        name="attend",
        compiler_params=pltpu.CompilerParams(vmem_limit_bytes=48 << 20),
    )(plan, docs, *qs, chosen)
    outs = [outs[0]] + [to_head(outs[j], j) for j in (1, 2, 3)]
    return pl.pallas_call(
        place, out_shape=(struct(32, 2048),) * 2, in_specs=[VMEM] * 4, out_specs=(VMEM,) * 2, name="place"
    )(*outs)


def solution(mesh):
    rows = P(("ctx", "head"), None)
    return jax.shard_map(
        on_device,
        mesh=mesh,
        in_specs=(rows,) * 6 + (P(), P()),
        out_specs=(rows, rows),
        check_vma=False,
    )
```

```python
import functools
import math

import jax
import jax.numpy as jnp
from jax import lax
from jax.experimental import pallas as pl
from jax.experimental.pallas import tpu as pltpu
from jax.sharding import PartitionSpec as P

HD = 128
BLK = 128
SHARDS = 64
PIECES = 16
WINDOW = 8
NEG = -1e30
SCALE = 1.0 / math.sqrt(HD)
LOG2E = math.log2(math.e)
BF = jnp.bfloat16
F32 = jnp.float32
VMEM = pl.BlockSpec(memory_space=pltpu.VMEM)
HBM = pl.BlockSpec(memory_space=pltpu.HBM)
SMEM = pl.BlockSpec(memory_space=pltpu.SMEM)


def lanes(start, size):
    return pl.ds(pl.multiple_of(start, 128), size)


def fetch_all(copies):
    for copy in copies:
        copy.start()
    for copy in copies:
        copy.wait()


def pack_keys(k, v, dk, dv, send):
    other = 1 - lax.axis_index("head") % 2
    for y in range(2):
        for a, ref in enumerate((k, v, dk, dv)):
            send[y, a] = ref[:, lanes((2 * y + other) * HD, HD)]


def pack_queries(q, dq, own, near, far, sems):
    h = lax.axis_index("head")
    copies = []
    for j, out in enumerate((own, near, far.at[0], far.at[1])):
        for i, ref in enumerate((q, dq)):
            source = ref.at[:, lanes(lax.bitwise_xor(h, j) * 512, 512)]
            copies.append(pltpu.make_async_copy(source, out.at[i], sems.at[len(copies)]))
    fetch_all(copies)


def spread(k, v, dk, dv, got, out):
    core = lax.axis_index("head") % 2
    for y in range(2):
        for a, ref in enumerate((k, v, dk, dv)):
            own = ref[:, lanes((2 * y + core) * HD, HD)]
            for r in range(4):
                at = 16 * (r % 2)
                piece = jnp.where(core == r // 2, own[at : at + 16], got[y, a, at : at + 16])
                for group in range(SHARDS // PIECES):
                    out[group * PIECES + a * 4 + r, y] = piece


def plan_sources(plan, docs, table, inverse):
    @pl.loop(0, SHARDS)
    def _(i):
        inverse[plan[i]] = i

    shard = lax.axis_index("ctx")
    group = shard // PIECES

    def fill(first, t, flags):
        doc = docs[t]
        for s in range(WINDOW):
            back = jnp.maximum(t - s, 0)
            same = jnp.logical_and(t >= s, docs[back] == doc)
            table[first + s] = same.astype(jnp.int32) if flags else inverse[jnp.where(same, back, t)]

    @pl.loop(0, PIECES)
    def _(d):
        fill(d * WINDOW, plan[group * PIECES + d], False)

    fill(PIECES * WINDOW, plan[shard], True)


def select(table, pieces, out):
    for d in range(PIECES):
        for s in range(WINDOW):
            out[d, s] = pieces[table[d * WINDOW + s]]


def attend(groups, table, keys, q_refs, o_refs):
    h = lax.axis_index("head")

    def gathered(a):
        return jnp.concatenate(
            [keys[a * 4 + r, s, y] for s in range(WINDOW) for y in range(2) for r in range(4)], axis=0
        )

    kk, vv, dkk, dvv = (gathered(a) for a in range(4))
    kdk = jnp.concatenate([kk, dkk], axis=1)
    vdv = jnp.concatenate([vv, dvv], axis=1)
    seen = [table[PIECES * WINDOW + s] == 1 for s in range(1, WINDOW)]
    contract_last = (((1,), (1,)), ((), ()))
    for j, q, o in zip(groups, q_refs, o_refs):
        qa = jnp.concatenate([q[0, :, g * HD : (g + 1) * HD] for g in range(4)], axis=0)
        dqa = jnp.concatenate([q[1, :, g * HD : (g + 1) * HD] for g in range(4)], axis=0)
        score = lax.dot_general(qa, kk, contract_last, preferred_element_type=F32)
        dscore = lax.dot_general(
            jnp.concatenate([dqa, qa], axis=1), kdk, contract_last, preferred_element_type=F32
        )
        row = lax.broadcasted_iota(jnp.int32, (128, 128), 0) % 32 + 32 * lax.bitwise_xor(h, j)
        col = lax.broadcasted_iota(jnp.int32, (128, 128), 1)
        parts = [jnp.where(col <= row, score[:, :BLK], NEG)]
        for s in range(1, WINDOW):
            parts.append(jnp.where(seen[s - 1], score[:, s * BLK : (s + 1) * BLK], NEG))
        masked = jnp.concatenate(parts, axis=1)
        top = jnp.max(masked, axis=1, keepdims=True)
        weight = jnp.exp2((masked - top) * (SCALE * LOG2E))
        total = jnp.sum(weight, axis=1, keepdims=True)
        wds = weight * dscore
        curve = jnp.sum(wds, axis=1, keepdims=True) * SCALE
        ab = jnp.dot(weight.astype(BF), vdv, preferred_element_type=F32)
        b1 = jnp.dot(wds.astype(BF), vv, preferred_element_type=F32)
        inv = 1.0 / total
        a = ab[:, :HD] * inv
        b = (b1 * SCALE + ab[:, HD:]) * inv - (curve * inv) * a
        ab_, bb_ = a.astype(BF), b.astype(BF)
        for g in range(4):
            o[0, :, g * HD : (g + 1) * HD] = ab_[g * 32 : (g + 1) * 32]
            o[1, :, g * HD : (g + 1) * HD] = bb_[g * 32 : (g + 1) * 32]


def attend_far(table, keys, direct, passed, out):
    attend((2, 3), table, keys, (direct.at[0], passed.at[1]), (out.at[0], out.at[1]))


def attend_near(table, keys, own, near, out_own, out_near):
    attend((0, 1), table, keys, (own, near), (out_own, out_near))


def place(own, near, direct, passed, att, tan):
    h = lax.axis_index("head")
    for j, r in enumerate((own, near, direct.at[0], passed.at[1])):
        at = lanes(lax.bitwise_xor(h, j) * 512, 512)
        att[:, at] = r[0]
        tan[:, at] = r[1]


def struct(*shape):
    return jax.ShapeDtypeStruct(shape, BF)


def to_head(value, j):
    return lax.ppermute(value, "head", [(i, i ^ j) for i in range(4)])


def call(body, out, *args, smem=0, limit=4, scratch=(), out_smem=False, source=VMEM, target=VMEM, cost=None):
    many = isinstance(out, tuple)
    place = SMEM if out_smem else target
    return pl.pallas_call(
        body,
        out_shape=out,
        in_specs=[SMEM] * smem + [source] * (len(args) - smem),
        out_specs=(place,) * len(out) if many else place,
        scratch_shapes=scratch,
        compiler_params=pltpu.CompilerParams(vmem_limit_bytes=limit << 20),
        cost_estimate=cost,
        name=body.__name__,
    )(*args)


def on_device(queries, key_rows, value_rows, query_tangent, key_tangent, value_tangent, plan, docs):
    rows = (key_rows, value_rows, key_tangent, value_tangent)
    got = to_head(call(pack_keys, struct(2, 4, 32, 128), *rows, limit=60), 1)
    pieces = call(spread, struct(SHARDS, 2, 16, 128), *rows, got)
    by_y = [[c * 4 + 2 * y + core for c in range(SHARDS) for y in range(2)] for core in range(2)]
    pieces = lax.all_to_all(
        pieces.reshape(SHARDS * 2, 16, 128), ("ctx", "head"), 0, 0, tiled=True, axis_index_groups=by_y
    ).reshape(SHARDS, 2, 16, 128)
    table = call(
        plan_sources,
        jax.ShapeDtypeStruct((PIECES * WINDOW + WINDOW,), jnp.int32),
        plan,
        docs,
        smem=2,
        out_smem=True,
        scratch=[pltpu.SMEM((SHARDS,), jnp.int32)],
        cost=pl.CostEstimate(flops=2_000_000_000, transcendentals=0, bytes_accessed=1_000_000),
    )
    own, near, far = call(
        pack_queries,
        (struct(2, 32, 512), struct(2, 32, 512), struct(2, 2, 32, 512)),
        queries,
        query_tangent,
        source=HBM,
        scratch=[pltpu.SemaphoreType.DMA((8,))],
    )
    far = to_head(far, 2)
    near = to_head(near, 1)
    far, near, table = lax.optimization_barrier((far, near, table))
    passed = to_head(far, 1)
    pieces, table, own, near, far, passed = lax.optimization_barrier((pieces, table, own, near, far, passed))
    chosen = call(select, struct(PIECES, WINDOW, 2, 16, 128), table, pieces, smem=1)
    groups = [[g * PIECES + i for i in range(PIECES)] for g in range(SHARDS // PIECES)]
    chosen = lax.all_to_all(
        chosen.reshape(PIECES, WINDOW * 32, 128), "ctx", 0, 0, tiled=True, axis_index_groups=groups
    ).reshape(PIECES, WINDOW, 2, 16, 128)
    cost = pl.CostEstimate(flops=400_000_000, transcendentals=262_144, bytes_accessed=1_500_000)
    far = call(attend_far, struct(2, 2, 32, 512), table, chosen, far, passed, smem=1, limit=24, cost=cost)
    chosen, own, near, far = lax.optimization_barrier((chosen, own, near, far))
    far = to_head(far, 2)
    own, near = call(attend_near, (struct(2, 32, 512),) * 2, table, chosen, own, near, smem=1, limit=24, cost=cost)
    near = to_head(near, 1)
    far, own, near = lax.optimization_barrier((far, own, near))
    passed = to_head(far, 1)
    return call(place, (struct(32, 2048),) * 2, own, near, far, passed)


def solution(mesh):
    rows = P(("ctx", "head"), None)
    return jax.shard_map(
        on_device,
        mesh=mesh,
        in_specs=(rows,) * 6 + (P(), P()),
        out_specs=(rows, rows),
        check_vma=False,
    )
```
